512 devices in a mesh: gx: 8 (over z), gy: 8 (over x, y_lo), gz: 8 (over y_hi, core).
Axes of the slice: x: 4, y: 8 (y_hi: 4, y_lo: 2; y = y_hi * 2 + y_lo), z: 8, core: 2. Of those that a mesh axis runs over, the one named last changes fastest.
Arguments:
- inputs: bfloat16 [512, 12288], P(('gx', 'gy'), 'gz'), may hold values from -6 to 6
- out_grad: bfloat16 [512, 12288], P(('gx', 'gy'), 'gz'), may hold values from -6 to 6
- preact: bfloat16 [512, 24576], P('gz', ('gx', 'gy')), may hold values from -6 to 6
- w_in: bfloat16 [12288, 24576], P('gz', ('gx', 'gy')), may hold values from -0.0546875 to 0.0546875
- w_out: bfloat16 [24576, 12288], P(('gx', 'gy'), 'gz'), may hold values from -0.0390625 to 0.0390625
Outputs:
- grad_input: bfloat16 [512, 12288], P(('gx', 'gy'), 'gz')
- grad_w_in: bfloat16 [12288, 24576], P('gz', ('gx', 'gy'))
- grad_w_out: bfloat16 [24576, 12288], P(('gx', 'gy'), 'gz')
The draws below stay inside these ranges and needn't reach their ends.
All inputs are finite; a program needn't handle non-finite values.
Results may differ from the reference program's by a relative error of at most 0.0049.
Values may be sent and summed in bfloat16 or wider, within the bound.
No kernel may reach another device: no remote copies, remote signals or barrier semaphores. Data moves between devices by JAX's collectives and lax.ppermute only.
A program may use at most 64 MiB of HBM per device.

```python
import jax
import jax.numpy as jnp

D = 12288
F = 24576
TOKENS = 512


def steps_of(stream_key, dims, split, low, high):
    def one(dim, blocks):
        steps = jax.random.uniform(jax.random.fold_in(jax.random.fold_in(stream_key, 6), dim), (blocks,), jnp.float32, low / len(split), high / len(split))
        return jnp.repeat(jnp.exp(steps), dims[dim] // blocks).reshape((-1,) + (1,) * (len(dims) - dim - 1))

    loudness = one(*split[0])
    for cut in split[1:]:
        loudness = loudness * one(*cut)
    return loudness


def scatter_about(key, dims, spread, bound, pieces=(), held_as=jnp.bfloat16):
    array = jax.random.normal(key, dims, jnp.float32) * spread
    if len(pieces) > 0:
        array = steps_of(key, dims, pieces, -0.22, 0.18) * array
    return jnp.clip(array, min=-bound, max=bound).astype(held_as)


def setup_inputs(seed: int = 0) -> dict:
    seeds = jax.random.split(jax.random.key(seed), 6)
    return {
        "inputs": scatter_about(seeds[0], (TOKENS, D), 1.0, 6.0, ((0, 64), (1, 8))),
        "out_grad": scatter_about(seeds[1], (TOKENS, D), 1.0, 6.0, ((0, 64), (1, 8))),
        "preact": scatter_about(seeds[2], (TOKENS, F), 1.5, 6.0, ((0, 8), (1, 64))),
        "w_in": scatter_about(seeds[3], (D, F), D ** -0.5, 0.0546875, ((0, 8), (1, 64))),
        "w_out": scatter_about(seeds[4], (F, D), F ** -0.5, 0.0390625, ((0, 64), (1, 8))),
    }


gelu_scale = 0.7978845608028654
cubic_coef = 0.044715


def gelu_parts(pre_float):
    tanh_arg = gelu_scale * (pre_float + cubic_coef * pre_float * pre_float * pre_float)
    tangent = jnp.tanh(tanh_arg)
    value = 0.5 * pre_float * (1.0 + tangent)
    slope = 0.5 * (1.0 + tangent) + 0.5 * pre_float * (1.0 - tangent * tangent) * gelu_scale * (1.0 + 3.0 * cubic_coef * pre_float * pre_float)
    return value, slope


def reference(inputs, out_grad, preact, w_in, w_out):
    value, slope = gelu_parts(preact.astype(jnp.float32))
    hidden = value.astype(jnp.bfloat16)
    grad_hidden = jnp.dot(out_grad, w_out.T, preferred_element_type=jnp.float32)
    grad_pre = (grad_hidden * slope).astype(jnp.bfloat16)
    grad_input = jnp.dot(grad_pre, w_in.T, preferred_element_type=jnp.float32).astype(jnp.bfloat16)
    grad_w_in = jnp.dot(inputs.T, grad_pre, preferred_element_type=jnp.float32).astype(jnp.bfloat16)
    grad_w_out = jnp.dot(hidden.T, out_grad, preferred_element_type=jnp.float32).astype(jnp.bfloat16)
    return grad_input, grad_w_in, grad_w_out
```

```python
import jax
import jax.numpy as jnp
from jax import lax
from jax.sharding import PartitionSpec as P

gelu_scale = 0.7978845608028654
cubic_coef = 0.044715


def gelu_parts(pre_float):
    tanh_arg = gelu_scale * (pre_float + cubic_coef * pre_float * pre_float * pre_float)
    tangent = jnp.tanh(tanh_arg)
    value = 0.5 * pre_float * (1.0 + tangent)
    slope = 0.5 * (1.0 + tangent) + 0.5 * pre_float * (1.0 - tangent * tangent) * gelu_scale * (
        1.0 + 3.0 * cubic_coef * pre_float * pre_float
    )
    return (value, slope)


def contract_rows(left, right):
    return lax.dot_general(
        left, right, (((1,), (1,)), ((), ())), preferred_element_type=jnp.float32
    )


def contract_cols(left, right):
    return lax.dot_general(
        left, right, (((0,), (0,)), ((), ())), preferred_element_type=jnp.float32
    )


def swap(blocks, axis):
    return lax.all_to_all(blocks, axis, split_axis=0, concat_axis=0, tiled=True)


def gather(block, axis, size):
    return swap(jnp.broadcast_to(block[None], (size,) + block.shape), axis)


def make(sizes):
    nx, ny, nz = sizes

    def on_device(inputs, out_grad, preact, w_in, w_out):
        tokens, width = inputs.shape
        rows_z, hidden_width = preact.shape
        total = nx * ny * tokens
        both = gather(jnp.stack([inputs, out_grad]), "gx", nx)
        rows_dy = gather(both[:, 1], "gy", ny).reshape(total, width)
        rows_x = gather(both[:, 0], "gy", ny).reshape(total, width)

        partial = contract_rows(rows_dy, w_out).astype(jnp.bfloat16)
        partial = partial.reshape(ny, nx, tokens, hidden_width).transpose(1, 0, 2, 3)
        partial = swap(partial.reshape(nz, rows_z, hidden_width), "gz")
        grad_hidden = jnp.sum(partial.astype(jnp.float32), axis=0)

        value_local, slope_local = gelu_parts(preact.astype(jnp.float32))
        grad_pre = (grad_hidden * slope_local).astype(jnp.bfloat16)
        hidden_local = value_local.astype(jnp.bfloat16)
        pair = gather(jnp.stack([grad_pre, hidden_local]), "gz", nz)

        def by_gy(block):
            block = block.reshape(nx, ny, tokens, hidden_width)
            return block.transpose(1, 0, 2, 3).reshape(total, hidden_width)

        grad_all, hidden_all = by_gy(pair[:, 0]), by_gy(pair[:, 1])

        part_in = contract_rows(grad_all, w_in).astype(jnp.bfloat16)
        part_in = swap(part_in.reshape(ny, nx * tokens, width), "gy")
        part_in = jnp.sum(part_in.astype(jnp.float32), axis=0).astype(jnp.bfloat16)
        part_in = swap(part_in.reshape(nx, tokens, width), "gx")
        grad_input = jnp.sum(part_in.astype(jnp.float32), axis=0).astype(jnp.bfloat16)

        grad_w_out = contract_cols(hidden_all, rows_dy).astype(jnp.bfloat16)
        grad_w_in = contract_cols(rows_x, grad_all).astype(jnp.bfloat16)
        return (grad_input, grad_w_in, grad_w_out)

    return on_device


def solution(mesh):
    in_specs = (
        P(("gx", "gy"), "gz"),
        P(("gx", "gy"), "gz"),
        P("gz", ("gx", "gy")),
        P("gz", ("gx", "gy")),
        P(("gx", "gy"), "gz"),
    )
    out_specs = (P(("gx", "gy"), "gz"), P("gz", ("gx", "gy")), P(("gx", "gy"), "gz"))
    sizes = tuple(mesh.shape[a] for a in ("gx", "gy", "gz"))
    return jax.shard_map(
        make(sizes), mesh=mesh, in_specs=in_specs, out_specs=out_specs, check_vma=False
    )
```

```python
import jax
import jax.numpy as jnp
from jax import lax
from jax.sharding import PartitionSpec as P

gelu_scale = 0.7978845608028654
cubic_coef = 0.044715


def gelu_parts(pre_float):
    tanh_arg = gelu_scale * (pre_float + cubic_coef * pre_float * pre_float * pre_float)
    tangent = jnp.tanh(tanh_arg)
    value = 0.5 * pre_float * (1.0 + tangent)
    slope = 0.5 * (1.0 + tangent) + 0.5 * pre_float * (1.0 - tangent * tangent) * gelu_scale * (
        1.0 + 3.0 * cubic_coef * pre_float * pre_float
    )
    return (value, slope)


def contract_rows(left, right):
    return lax.dot_general(
        left, right, (((1,), (1,)), ((), ())), preferred_element_type=jnp.float32
    )


def contract_cols(left, right):
    return lax.dot_general(
        left, right, (((0,), (0,)), ((), ())), preferred_element_type=jnp.float32
    )


def swap(blocks, axis):
    return lax.all_to_all(blocks, axis, split_axis=0, concat_axis=0, tiled=True)


def gather(block, axis, size):
    return swap(jnp.broadcast_to(block[None], (size,) + block.shape), axis)


def add_up(blocks):
    parts = [blocks[i].astype(jnp.float32) for i in range(blocks.shape[0])]
    while len(parts) > 1:
        parts = [
            parts[i] + parts[i + 1] if i + 1 < len(parts) else parts[i]
            for i in range(0, len(parts), 2)
        ]
    return parts[0]


def make(sizes):
    nx, ny, nz = sizes

    def on_device(inputs, out_grad, preact, w_in, w_out):
        tokens, width = inputs.shape
        rows_z, hidden_width = preact.shape
        total = nx * ny * tokens
        span = nx * tokens
        near_dy = gather(out_grad, "gx", nx).reshape(span, width)
        both = gather(jnp.concatenate([near_dy, inputs]), "gy", ny)
        rows_dy = both[:, :span].reshape(total, width)
        near_x = both[:, span:].reshape(ny * tokens, width)
        rows_x = lax.all_gather(near_x, "gx", axis=0, tiled=True)

        def turn(block, outer, inner):
            block = block.reshape(outer, inner, tokens, -1)
            return block.transpose(1, 0, 2, 3).reshape(total, -1)

        partial = contract_rows(rows_dy, w_out).astype(jnp.bfloat16)
        partial = turn(partial, ny, nx)
        grad_hidden = add_up(swap(partial.reshape(nz, rows_z, hidden_width), "gz"))

        value_local, slope_local = gelu_parts(preact.astype(jnp.float32))
        grad_pre = (grad_hidden * slope_local).astype(jnp.bfloat16)
        hidden_local = value_local.astype(jnp.bfloat16)
        pair = lax.all_gather(
            jnp.concatenate([grad_pre, hidden_local], axis=1), "gz", axis=0, tiled=True
        )
        grad_all, hidden_all = pair[:, :hidden_width], pair[:, hidden_width:]

        part_in = contract_rows(turn(grad_all, nx, ny), w_in).astype(jnp.bfloat16)
        part_in = swap(part_in.reshape(ny, span, width), "gy")
        grad_w_in = contract_cols(rows_x, grad_all).astype(jnp.bfloat16)
        part_in, grad_w_in = lax.optimization_barrier((part_in, grad_w_in))
        part_in = add_up(part_in)
        part_in = part_in.astype(jnp.bfloat16).reshape(nx, tokens, width)
        grad_input = add_up(swap(part_in, "gx")).astype(jnp.bfloat16)

        grad_w_out = contract_cols(turn(hidden_all, nx, ny), rows_dy)
        return (
            grad_input,
            grad_w_in,
            grad_w_out.astype(jnp.bfloat16),
        )

    return on_device


def solution(mesh):
    in_specs = (
        P(("gx", "gy"), "gz"),
        P(("gx", "gy"), "gz"),
        P("gz", ("gx", "gy")),
        P("gz", ("gx", "gy")),
        P(("gx", "gy"), "gz"),
    )
    out_specs = (P(("gx", "gy"), "gz"), P("gz", ("gx", "gy")), P(("gx", "gy"), "gz"))
    sizes = tuple(mesh.shape[a] for a in ("gx", "gy", "gz"))
    return jax.shard_map(
        make(sizes), mesh=mesh, in_specs=in_specs, out_specs=out_specs, check_vma=False
    )
```

```python
import jax
import jax.numpy as jnp
from jax import lax
from jax.sharding import Mesh
from jax.sharding import PartitionSpec as P

gelu_scale = 0.7978845608028654
cubic_coef = 0.044715


def gelu_parts(pre_float):
    tanh_arg = gelu_scale * (pre_float + cubic_coef * pre_float * pre_float * pre_float)
    tangent = jnp.tanh(tanh_arg)
    value = 0.5 * pre_float * (1.0 + tangent)
    slope = 0.5 * (1.0 + tangent) + 0.5 * pre_float * (1.0 - tangent * tangent) * gelu_scale * (
        1.0 + 3.0 * cubic_coef * pre_float * pre_float
    )
    return (value, slope)


def contract_rows(left, right):
    return lax.dot_general(
        left, right, (((1,), (1,)), ((), ())), preferred_element_type=jnp.float32
    )


def contract_cols(left, right):
    return lax.dot_general(
        left, right, (((0,), (0,)), ((), ())), preferred_element_type=jnp.float32
    )


def swap(blocks, axis):
    return lax.all_to_all(blocks, axis, split_axis=0, concat_axis=0, tiled=True)


def gather(block, axis, size):
    return swap(jnp.broadcast_to(block[None], (size,) + block.shape), axis)


def add_up(blocks):
    parts = [blocks[i].astype(jnp.float32) for i in range(blocks.shape[0])]
    while len(parts) > 1:
        parts = [
            parts[i] + parts[i + 1] if i + 1 < len(parts) else parts[i]
            for i in range(0, len(parts), 2)
        ]
    return parts[0]


def make(sizes):
    nx, ny, nh, nc = sizes

    def on_device(inputs, out_grad, preact, w_in, w_out):
        tokens, width = inputs.shape
        rows_z, hidden_width = preact.shape
        total = nx * ny * tokens
        span = nx * tokens
        out_grad, first = lax.optimization_barrier((out_grad, lax.axis_index("gc") == 0))
        near_dy = gather(out_grad, "gx", nx).reshape(span, width)
        both = gather(jnp.concatenate([near_dy, inputs]), "gy", ny)
        rows_dy = both[:, :span].reshape(total, width)
        near_x = both[:, span:].reshape(ny * tokens, width)
        rows_x = lax.all_gather(near_x, "gx", axis=0, tiled=True)

        partial = contract_rows(rows_dy, w_out)
        partial = partial.reshape(ny, nh, nc, tokens, hidden_width)
        partial = partial.transpose(2, 1, 0, 3, 4).reshape(nc, nh * rows_z, hidden_width)
        theirs = jnp.where(first, partial[1], partial[0])
        mine = jnp.where(first, partial[0], partial[1])
        theirs = lax.all_gather(theirs, "gc", axis=0)
        mine = mine + jnp.where(first, theirs[1], theirs[0])
        chips = lax.all_gather(
            jnp.concatenate([mine.astype(jnp.bfloat16), preact]), "gh", axis=0
        )
        grad_hidden = add_up(chips[:, : nh * rows_z])
        pre = chips[:, nh * rows_z :].reshape(nh * rows_z, hidden_width)

        value, slope = gelu_parts(pre.astype(jnp.float32))
        grad_pre = (grad_hidden * slope).astype(jnp.bfloat16)
        pair = lax.all_gather(
            jnp.concatenate([grad_pre, value.astype(jnp.bfloat16)], axis=1), "gc", axis=0
        )
        pair = pair.reshape(nc, nh, ny, tokens, 2 * hidden_width)

        def by_gx(block):
            return block.transpose(1, 0, 2, 3, 4).reshape(total, hidden_width)

        def by_gy(block):
            return block.transpose(2, 1, 0, 3, 4).reshape(total, hidden_width)

        grad_all, hidden_all = pair[..., :hidden_width], pair[..., hidden_width:]

        part_in = contract_rows(by_gy(grad_all), w_in).astype(jnp.bfloat16)
        part_in = swap(part_in.reshape(ny, span, width), "gy")
        grad_w_in = contract_cols(rows_x, by_gx(grad_all)).astype(jnp.bfloat16)
        grad_w_out = contract_cols(by_gy(hidden_all), rows_dy).astype(jnp.bfloat16)
        part_in, grad_w_in, grad_w_out = lax.optimization_barrier(
            (part_in, grad_w_in, grad_w_out)
        )
        part_in = add_up(part_in)
        part_in = part_in.astype(jnp.bfloat16).reshape(nx, tokens, width)
        grad_input = add_up(swap(part_in, "gx")).astype(jnp.bfloat16)
        return (grad_input, grad_w_in, grad_w_out)

    return on_device


def solution(mesh):
    nx, ny, nz = (mesh.shape[a] for a in ("gx", "gy", "gz"))
    nc = 2
    sizes = (nx, ny, nz // nc, nc)
    mesh = Mesh(mesh.devices.reshape(sizes), ("gx", "gy", "gh", "gc"))
    tokens, features = ("gx", "gy"), ("gh", "gc")
    in_specs = (
        P(tokens, features),
        P(tokens, features),
        P(features, tokens),
        P(features, tokens),
        P(tokens, features),
    )
    out_specs = (P(tokens, features), P(features, tokens), P(tokens, features))
    return jax.shard_map(
        make(sizes), mesh=mesh, in_specs=in_specs, out_specs=out_specs, check_vma=False
    )
```

```python
import jax
import jax.numpy as jnp
from jax import lax
from jax.sharding import Mesh
from jax.sharding import PartitionSpec as P

gelu_scale = 0.7978845608028654
cubic_coef = 0.044715


def gelu_parts(pre_float):
    tanh_arg = gelu_scale * (pre_float + cubic_coef * pre_float * pre_float * pre_float)
    tangent = jnp.tanh(tanh_arg)
    value = 0.5 * pre_float * (1.0 + tangent)
    slope = 0.5 * (1.0 + tangent) + 0.5 * pre_float * (1.0 - tangent * tangent) * gelu_scale * (
        1.0 + 3.0 * cubic_coef * pre_float * pre_float
    )
    return (value, slope)


def contract_rows(left, right):
    return lax.dot_general(
        left, right, (((1,), (1,)), ((), ())), preferred_element_type=jnp.float32
    )


def contract_cols(left, right):
    return lax.dot_general(
        left, right, (((0,), (0,)), ((), ())), preferred_element_type=jnp.float32
    )


def swap(blocks, axis):
    return lax.all_to_all(blocks, axis, split_axis=0, concat_axis=0, tiled=True)


def gather(block, axis, size):
    return swap(jnp.broadcast_to(block[None], (size,) + block.shape), axis)


def add_up(blocks):
    parts = [blocks[i].astype(jnp.float32) for i in range(blocks.shape[0])]
    while len(parts) > 1:
        parts = [
            parts[i] + parts[i + 1] if i + 1 < len(parts) else parts[i]
            for i in range(0, len(parts), 2)
        ]
    return parts[0]


def make(sizes):
    nx, ny, nh, nc = sizes

    def on_device(inputs, out_grad, preact, w_in, w_out):
        tokens, width = inputs.shape
        rows_z, hidden_width = preact.shape
        total = nx * ny * tokens
        span = nx * tokens
        own, first = lax.optimization_barrier(
            (jnp.stack([out_grad, inputs]), lax.axis_index("gc") == 0)
        )
        near_dy = gather(own[0], "gx", nx).reshape(span, width)
        both = gather(jnp.concatenate([near_dy, own[1]]), "gy", ny)
        rows_dy = both[:, :span].reshape(total, width)
        near_x = both[:, span:].reshape(ny * tokens, width)
        rows_x = lax.all_gather(near_x, "gx", axis=0, tiled=True)

        partial = contract_rows(rows_dy, w_out)
        partial = partial.reshape(ny, nh, nc, tokens, hidden_width)
        partial = partial.transpose(2, 1, 0, 3, 4).reshape(nc, nh * rows_z, hidden_width)
        theirs = jnp.where(first, partial[1], partial[0])
        mine = jnp.where(first, partial[0], partial[1])
        theirs = lax.all_gather(theirs, "gc", axis=0)
        mine = mine + jnp.where(first, theirs[1], theirs[0])
        chips = lax.all_gather(
            jnp.concatenate([mine.astype(jnp.bfloat16), preact]), "gh", axis=0
        )
        grad_hidden = add_up(chips[:, : nh * rows_z])
        pre = chips[:, nh * rows_z :].reshape(nh * rows_z, hidden_width)

        value, slope = gelu_parts(pre.astype(jnp.float32))
        grad_pre = (grad_hidden * slope).astype(jnp.bfloat16)
        pair = lax.all_gather(
            jnp.concatenate([grad_pre, value.astype(jnp.bfloat16)], axis=1), "gc", axis=0
        )
        pair = pair.reshape(nc, nh, ny, tokens, 2 * hidden_width)

        def by_gx(block):
            return block.transpose(1, 0, 2, 3, 4).reshape(total, hidden_width)

        def by_gy(block):
            return block.transpose(2, 1, 0, 3, 4).reshape(total, hidden_width)

        grad_all, hidden_all = pair[..., :hidden_width], pair[..., hidden_width:]

        part_in = contract_rows(by_gy(grad_all), w_in).astype(jnp.bfloat16)
        part_in = swap(part_in.reshape(ny, span, width), "gy")
        grad_w_in = contract_cols(rows_x, by_gx(grad_all)).astype(jnp.bfloat16)
        grad_w_out = contract_cols(by_gy(hidden_all), rows_dy).astype(jnp.bfloat16)
        part_in, grad_w_in, grad_w_out = lax.optimization_barrier(
            (part_in, grad_w_in, grad_w_out)
        )
        part_in = add_up(part_in)
        part_in = part_in.astype(jnp.bfloat16).reshape(nx, tokens, width)
        grad_input = add_up(swap(part_in, "gx")).astype(jnp.bfloat16)
        return (grad_input, grad_w_in, grad_w_out)

    return on_device


def solution(mesh):
    nx, ny, nz = (mesh.shape[a] for a in ("gx", "gy", "gz"))
    nc = 2
    sizes = (nx, ny, nz // nc, nc)
    mesh = Mesh(mesh.devices.reshape(sizes), ("gx", "gy", "gh", "gc"))
    tokens, features = ("gx", "gy"), ("gh", "gc")
    in_specs = (
        P(tokens, features),
        P(tokens, features),
        P(features, tokens),
        P(features, tokens),
        P(tokens, features),
    )
    out_specs = (P(tokens, features), P(features, tokens), P(tokens, features))
    return jax.shard_map(
        make(sizes), mesh=mesh, in_specs=in_specs, out_specs=out_specs, check_vma=False
    )
```

```python
import jax
import jax.numpy as jnp
from jax import lax
from jax.sharding import Mesh
from jax.sharding import PartitionSpec as P

gelu_scale = 0.7978845608028654
cubic_coef = 0.044715


def gelu_parts(pre_float):
    tanh_arg = gelu_scale * (pre_float + cubic_coef * pre_float * pre_float * pre_float)
    tangent = jnp.tanh(tanh_arg)
    value = 0.5 * pre_float * (1.0 + tangent)
    slope = 0.5 * (1.0 + tangent) + 0.5 * pre_float * (1.0 - tangent * tangent) * gelu_scale * (
        1.0 + 3.0 * cubic_coef * pre_float * pre_float
    )
    return (value, slope)


def contract_rows(left, right):
    return lax.dot_general(
        left, right, (((1,), (1,)), ((), ())), preferred_element_type=jnp.float32
    )


def contract_cols(left, right):
    return lax.dot_general(
        left, right, (((0,), (0,)), ((), ())), preferred_element_type=jnp.float32
    )


def swap(blocks, axis):
    return lax.all_to_all(blocks, axis, split_axis=0, concat_axis=0, tiled=True)


def gather(block, axis, size):
    return swap(jnp.broadcast_to(block[None], (size,) + block.shape), axis)


def add_up(blocks):
    parts = [blocks[i].astype(jnp.float32) for i in range(blocks.shape[0])]
    while len(parts) > 1:
        parts = [
            parts[i] + parts[i + 1] if i + 1 < len(parts) else parts[i]
            for i in range(0, len(parts), 2)
        ]
    return parts[0]


def make(sizes):
    nx, ny, nh, nc = sizes

    def on_device(inputs, out_grad, preact, w_in, w_out):
        tokens, width = inputs.shape
        rows_z, hidden_width = preact.shape
        total = nx * ny * tokens
        span = nx * tokens
        own, first = lax.optimization_barrier(
            (jnp.stack([out_grad, inputs]), lax.axis_index("gc") == 0)
        )
        near_dy = gather(own[0], "gx", nx).reshape(span, width)
        both = gather(jnp.concatenate([near_dy, own[1]]), "gy", ny)
        rows_dy = both[:, :span].reshape(total, width)
        near_x = both[:, span:].reshape(ny * tokens, width)
        rows_x = gather(near_x, "gx", nx).reshape(total, width)

        partial = contract_rows(rows_dy, w_out)
        partial = partial.reshape(ny, nh, nc, tokens, hidden_width)
        partial = partial.transpose(2, 1, 0, 3, 4).reshape(nc, nh * rows_z, hidden_width)
        theirs = jnp.where(first, partial[1], partial[0])
        mine = jnp.where(first, partial[0], partial[1])
        theirs = lax.all_gather(theirs, "gc", axis=0)
        mine = mine + jnp.where(first, theirs[1], theirs[0])
        chips = lax.all_gather(
            jnp.concatenate([mine.astype(jnp.bfloat16), preact]), "gh", axis=0
        )
        grad_hidden = add_up(chips[:, : nh * rows_z])
        pre = chips[:, nh * rows_z :].reshape(nh * rows_z, hidden_width)

        value, slope = gelu_parts(pre.astype(jnp.float32))
        grad_pre = (grad_hidden * slope).astype(jnp.bfloat16)
        pair = lax.all_gather(
            jnp.concatenate([grad_pre, value.astype(jnp.bfloat16)], axis=1), "gc", axis=0
        )
        pair = pair.reshape(nc, nh, ny, tokens, 2 * hidden_width)

        def by_gx(block):
            return block.transpose(1, 0, 2, 3, 4).reshape(total, hidden_width)

        def by_gy(block):
            return block.transpose(2, 1, 0, 3, 4).reshape(total, hidden_width)

        grad_all, hidden_all = pair[..., :hidden_width], pair[..., hidden_width:]

        part_in = contract_rows(by_gy(grad_all), w_in).astype(jnp.bfloat16)
        part_in = swap(part_in.reshape(ny, span, width), "gy")
        grad_w_in = contract_cols(rows_x, by_gx(grad_all)).astype(jnp.bfloat16)
        grad_w_out = contract_cols(by_gy(hidden_all), rows_dy).astype(jnp.bfloat16)
        part_in, grad_w_in, grad_w_out = lax.optimization_barrier(
            (part_in, grad_w_in, grad_w_out)
        )
        part_in = add_up(part_in)
        part_in = part_in.astype(jnp.bfloat16).reshape(nx, tokens, width)
        grad_input = add_up(swap(part_in, "gx")).astype(jnp.bfloat16)
        return (grad_input, grad_w_in, grad_w_out)

    return on_device


def solution(mesh):
    nx, ny, nz = (mesh.shape[a] for a in ("gx", "gy", "gz"))
    nc = 2
    sizes = (nx, ny, nz // nc, nc)
    mesh = Mesh(mesh.devices.reshape(sizes), ("gx", "gy", "gh", "gc"))
    tokens, features = ("gx", "gy"), ("gh", "gc")
    in_specs = (
        P(tokens, features),
        P(tokens, features),
        P(features, tokens),
        P(features, tokens),
        P(tokens, features),
    )
    out_specs = (P(tokens, features), P(features, tokens), P(tokens, features))
    return jax.shard_map(
        make(sizes), mesh=mesh, in_specs=in_specs, out_specs=out_specs, check_vma=False
    )
```

```python
import jax
import jax.numpy as jnp
from jax import lax
from jax.sharding import Mesh
from jax.sharding import PartitionSpec as P

gelu_scale = 0.7978845608028654
cubic_coef = 0.044715


def gelu_parts(pre_float):
    tanh_arg = gelu_scale * (pre_float + cubic_coef * pre_float * pre_float * pre_float)
    tangent = jnp.tanh(tanh_arg)
    value = 0.5 * pre_float * (1.0 + tangent)
    slope = 0.5 * (1.0 + tangent) + 0.5 * pre_float * (1.0 - tangent * tangent) * gelu_scale * (
        1.0 + 3.0 * cubic_coef * pre_float * pre_float
    )
    return (value, slope)


def contract_rows(left, right):
    return lax.dot_general(
        left, right, (((1,), (1,)), ((), ())), preferred_element_type=jnp.float32
    )


def contract_cols(left, right):
    return lax.dot_general(
        left, right, (((0,), (0,)), ((), ())), preferred_element_type=jnp.float32
    )


def swap(blocks, axis):
    return lax.all_to_all(blocks, axis, split_axis=0, concat_axis=0, tiled=True)


def gather(block, axis, size):
    return swap(jnp.broadcast_to(block[None], (size,) + block.shape), axis)


def add_up(blocks):
    parts = [blocks[i].astype(jnp.float32) for i in range(blocks.shape[0])]
    while len(parts) > 1:
        parts = [
            parts[i] + parts[i + 1] if i + 1 < len(parts) else parts[i]
            for i in range(0, len(parts), 2)
        ]
    return parts[0]


def make(sizes):
    nx, ny, nh, nc = sizes

    def on_device(inputs, out_grad, preact, w_in, w_out):
        tokens, width = inputs.shape
        rows_z, hidden_width = preact.shape
        total = nx * ny * tokens
        span = nx * tokens
        own, first = lax.optimization_barrier(
            (jnp.stack([out_grad, inputs]), lax.axis_index("gc") == 0)
        )
        near_dy = gather(own[0], "gx", nx).reshape(span, width)
        both = gather(jnp.concatenate([near_dy, own[1]]), "gy", ny)
        rows_dy, both = lax.optimization_barrier((both[:, :span], both))
        rows_dy = rows_dy.reshape(total, width)
        near_x = both[:, span:].reshape(ny * tokens, width)
        rows_x = gather(near_x, "gx", nx).reshape(total, width)

        partial = contract_rows(rows_dy, w_out)
        partial = partial.reshape(ny, nh, nc, tokens, hidden_width)
        partial = partial.transpose(2, 1, 0, 3, 4).reshape(nc, nh * rows_z, hidden_width)
        theirs = jnp.where(first, partial[1], partial[0])
        mine = jnp.where(first, partial[0], partial[1])
        theirs = lax.all_gather(theirs, "gc", axis=0)
        mine = mine + jnp.where(first, theirs[1], theirs[0])
        chips = lax.all_gather(
            jnp.concatenate([mine.astype(jnp.bfloat16), preact]), "gh", axis=0
        )
        grad_hidden = add_up(chips[:, : nh * rows_z])
        pre = chips[:, nh * rows_z :].reshape(nh * rows_z, hidden_width)

        value, slope = gelu_parts(pre.astype(jnp.float32))
        grad_pre = (grad_hidden * slope).astype(jnp.bfloat16)
        pair = lax.all_gather(
            jnp.concatenate([grad_pre, value.astype(jnp.bfloat16)], axis=1), "gc", axis=0
        )
        pair = pair.reshape(nc, nh, ny, tokens, 2 * hidden_width)

        def by_gx(block):
            return block.transpose(1, 0, 2, 3, 4).reshape(total, hidden_width)

        def by_gy(block):
            return block.transpose(2, 1, 0, 3, 4).reshape(total, hidden_width)

        grad_all, hidden_all = pair[..., :hidden_width], pair[..., hidden_width:]

        part_in = contract_rows(by_gy(grad_all), w_in).astype(jnp.bfloat16)
        part_in = swap(part_in.reshape(ny, span, width), "gy")
        grad_w_in = contract_cols(rows_x, by_gx(grad_all)).astype(jnp.bfloat16)
        grad_w_out = contract_cols(by_gy(hidden_all), rows_dy).astype(jnp.bfloat16)
        part_in, grad_w_in, grad_w_out = lax.optimization_barrier(
            (part_in, grad_w_in, grad_w_out)
        )
        part_in = add_up(part_in)
        part_in = part_in.astype(jnp.bfloat16).reshape(nx, tokens, width)
        grad_input = add_up(swap(part_in, "gx")).astype(jnp.bfloat16)
        return (grad_input, grad_w_in, grad_w_out)

    return on_device


def solution(mesh):
    nx, ny, nz = (mesh.shape[a] for a in ("gx", "gy", "gz"))
    nc = 2
    sizes = (nx, ny, nz // nc, nc)
    mesh = Mesh(mesh.devices.reshape(sizes), ("gx", "gy", "gh", "gc"))
    tokens, features = ("gx", "gy"), ("gh", "gc")
    in_specs = (
        P(tokens, features),
        P(tokens, features),
        P(features, tokens),
        P(features, tokens),
        P(tokens, features),
    )
    out_specs = (P(tokens, features), P(features, tokens), P(tokens, features))
    return jax.shard_map(
        make(sizes), mesh=mesh, in_specs=in_specs, out_specs=out_specs, check_vma=False
    )
```

```python
import jax
import jax.numpy as jnp
from jax import lax
from jax.sharding import Mesh
from jax.sharding import PartitionSpec as P

gelu_scale = 0.7978845608028654
cubic_coef = 0.044715


def gelu_parts(pre_float):
    tanh_arg = gelu_scale * (pre_float + cubic_coef * pre_float * pre_float * pre_float)
    tangent = jnp.tanh(tanh_arg)
    value = 0.5 * pre_float * (1.0 + tangent)
    slope = 0.5 * (1.0 + tangent) + 0.5 * pre_float * (1.0 - tangent * tangent) * gelu_scale * (
        1.0 + 3.0 * cubic_coef * pre_float * pre_float
    )
    return (value, slope)


def contract_rows(left, right):
    return lax.dot_general(
        left, right, (((1,), (1,)), ((), ())), preferred_element_type=jnp.float32
    )


def contract_cols(left, right):
    return lax.dot_general(
        left, right, (((0,), (0,)), ((), ())), preferred_element_type=jnp.float32
    )


def swap(blocks, axis):
    return lax.all_to_all(blocks, axis, split_axis=0, concat_axis=0, tiled=True)


def gather(block, axis, size):
    return swap(jnp.broadcast_to(block[None], (size,) + block.shape), axis)


def add_up(blocks):
    parts = [blocks[i].astype(jnp.float32) for i in range(blocks.shape[0])]
    while len(parts) > 1:
        parts = [
            parts[i] + parts[i + 1] if i + 1 < len(parts) else parts[i]
            for i in range(0, len(parts), 2)
        ]
    return parts[0]


def make(sizes):
    nx, ny, nh, nc = sizes

    def on_device(inputs, out_grad, preact, w_in, w_out):
        tokens, width = inputs.shape
        rows_z, hidden_width = preact.shape
        total = nx * ny * tokens
        span = nx * tokens
        own, first = lax.optimization_barrier(
            (jnp.stack([out_grad, inputs]), lax.axis_index("gc") == 0)
        )
        near_dy = gather(own[0], "gx", nx).reshape(span, width)
        both = gather(jnp.concatenate([near_dy, own[1]]), "gy", ny)
        rows_dy, both = lax.optimization_barrier((both[:, :span], both))
        rows_dy = rows_dy.reshape(total, width)
        near_x = both[:, span:].reshape(ny * tokens, width)
        rows_x = gather(near_x, "gx", nx).reshape(total, width)

        partial = contract_rows(rows_dy, w_out)
        partial = partial.reshape(ny, nh, nc, tokens, hidden_width)
        partial = partial.transpose(2, 1, 0, 3, 4).reshape(nc, nh * rows_z, hidden_width)
        theirs = jnp.where(first, partial[1], partial[0])
        mine = jnp.where(first, partial[0], partial[1])
        theirs = lax.all_gather(theirs, "gc", axis=0)
        mine = mine + jnp.where(first, theirs[1], theirs[0])
        chips = lax.all_gather(
            jnp.concatenate([mine.astype(jnp.bfloat16), preact]), "gh", axis=0
        )
        grad_hidden = add_up(chips[:, : nh * rows_z])
        pre = chips[:, nh * rows_z :].reshape(nh * rows_z, hidden_width)

        _, slope = gelu_parts(pre.astype(jnp.float32))
        grad_pre = (grad_hidden * slope).astype(jnp.bfloat16)
        grad_all = lax.all_gather(grad_pre, "gc", axis=0)
        grad_all = grad_all.reshape(nc, nh, ny, tokens, hidden_width)

        def by_gx(block):
            return block.transpose(1, 0, 2, 3, 4).reshape(total, hidden_width)

        def by_gy(block):
            return block.transpose(2, 1, 0, 3, 4).reshape(total, hidden_width)

        part_in = contract_rows(by_gy(grad_all), w_in).astype(jnp.bfloat16)
        part_in, pre = lax.optimization_barrier((part_in, pre))
        value, _ = gelu_parts(pre.astype(jnp.float32))
        hidden_all = lax.all_gather(value.astype(jnp.bfloat16), "gc", axis=0)
        hidden_all = hidden_all.reshape(nc, nh, ny, tokens, hidden_width)
        part_in = swap(part_in.reshape(ny, span, width), "gy")
        grad_w_in = contract_cols(rows_x, by_gx(grad_all)).astype(jnp.bfloat16)
        grad_w_out = contract_cols(by_gy(hidden_all), rows_dy).astype(jnp.bfloat16)
        part_in, grad_w_in, grad_w_out = lax.optimization_barrier(
            (part_in, grad_w_in, grad_w_out)
        )
        part_in = add_up(part_in)
        part_in = part_in.astype(jnp.bfloat16).reshape(nx, tokens, width)
        grad_input = add_up(swap(part_in, "gx")).astype(jnp.bfloat16)
        return (grad_input, grad_w_in, grad_w_out)

    return on_device


def solution(mesh):
    nx, ny, nz = (mesh.shape[a] for a in ("gx", "gy", "gz"))
    nc = 2
    sizes = (nx, ny, nz // nc, nc)
    mesh = Mesh(mesh.devices.reshape(sizes), ("gx", "gy", "gh", "gc"))
    tokens, features = ("gx", "gy"), ("gh", "gc")
    in_specs = (
        P(tokens, features),
        P(tokens, features),
        P(features, tokens),
        P(features, tokens),
        P(tokens, features),
    )
    out_specs = (P(tokens, features), P(features, tokens), P(tokens, features))
    return jax.shard_map(
        make(sizes), mesh=mesh, in_specs=in_specs, out_specs=out_specs, check_vma=False
    )
```
